32 devices in a mesh: sec: 4 (over x, core), dp: 2 (over y), mp: 4 (over z).
Axes of the slice: x: 2, y: 2, z: 4, core: 2. Of those that a mesh axis runs over, the one named last changes fastest.
Arguments:
- queries: bfloat16 [1024, 8192], P(('sec', 'dp'), 'mp'), may hold values from -6 to 6
- cotangent: bfloat16 [1024, 8192], P(('sec', 'dp'), 'mp'), may hold values from -6 to 6
- keys_raw: bfloat16 [80, 48, 1024], P(('sec', 'dp'), None, 'mp'), may hold values from -6 to 6
- values: bfloat16 [80, 48, 1024], P(('sec', 'dp'), None, 'mp'), may hold values from -6 to 6
- image_counts: int32 [32], P(('sec', 'dp')), may hold values from 1 to 4, as said below
- image_route: int32 [80], P(('sec', 'dp')), may hold values from 0 to 127, as said below
- text_lengths: int32 [32], P(('sec', 'dp')), may hold values from 1 to 32, as said below
- q_gain: float32 [128], replicated
- k_gain: float32 [128], replicated
Outputs:
- query_grad: bfloat16 [1024, 8192], P(('sec', 'dp'), 'mp')
- key_grad: bfloat16 [80, 48, 1024], P(('sec', 'dp'), None, 'mp')
- value_grad: bfloat16 [80, 48, 1024], P(('sec', 'dp'), None, 'mp')
- q_gain_grad: float32 [128], replicated
- k_gain_grad: float32 [128], replicated
The draws below stay inside these ranges and needn't reach their ends.
Inputs may be any that keep to these rules, and one draw needn't show every extreme that they name: `image_counts`: the counts of the 8 sequences of one index of sec sum to 20. `image_route`: each pair (s, k) with k < image_counts[s] appears exactly once; the images of an index of sec belong to sequences of that index; of the images of one device, at most 8 belong to the sequences of any one device, and this is reached. `text_lengths`: some sequence of every device has 32 live tokens.
All inputs are finite; a program needn't handle non-finite values.
Results may differ from the reference program's by a relative error of at most 0.01.
The reference program's roundings to bfloat16 on the way (of `key_norm`, `query_norm`, `slot_keys`, `probs_low`, `grad`, `dscore` and `dk_slots`) count: a program that leaves them out, or rounds other values in their place, can miss the bound.
Values may be sent and summed in bfloat16 or wider, within the bound.
A program may use at most 64 MiB of HBM per device.

```python
import math
import jax
import jax.numpy as jnp
from jax import lax

H = 64
KVH = 8
HD = 128
SEQ_DEV = 4
LEN = 32
PATCH = 48
GROUP = 8
GROUP_SEQS = 8
SEQS = 32
IMG_DEV = 10
GROUP_IMAGES = 20
IMAGES = 80
TOKENS = 1024


def shuffle_row(row_key, row):
    return jax.random.permutation(row_key, row)


def counts_and_route(key):
    sections = SEQS // GROUP_SEQS
    dp_count = GROUP_SEQS // SEQ_DEV
    half = GROUP_SEQS // 2
    first = jax.random.randint(jax.random.fold_in(key, 11), (sections, half), 1, 5)
    first = first.at[:, 0].set(4)
    paired = jnp.concatenate([first, 5 - first], axis=1)
    row_keys = jax.random.split(jax.random.fold_in(key, 12), sections)
    shuffled = jax.vmap(shuffle_row)(row_keys, paired).astype(jnp.int32)
    section_ids = jnp.arange(sections, dtype=jnp.int32)
    top_place = jnp.argmax(shuffled, axis=1).astype(jnp.int32)
    last_count = shuffled[:, GROUP_SEQS - 1]
    shuffled = shuffled.at[section_ids, top_place].set(last_count)
    shuffled = shuffled.at[:, GROUP_SEQS - 1].set(4)
    ends = jnp.cumsum(shuffled, axis=1)
    starts = ends - shuffled
    image_pos = jnp.arange(GROUP_IMAGES, dtype=jnp.int32)
    seq_local = jnp.sum((image_pos[None, :, None] >= ends[:, None, :]).astype(jnp.int32), axis=2)
    within = image_pos[None, :] - jnp.take_along_axis(starts, seq_local, axis=1)
    seq_global = seq_local + (section_ids * GROUP_SEQS)[:, None]
    codes = 4 * seq_global + within
    source_keys = jax.random.split(jax.random.fold_in(key, 13), sections)
    base_rows = jnp.broadcast_to(jnp.arange(dp_count, dtype=jnp.int32), (sections, dp_count))
    source_perm = jax.vmap(shuffle_row)(source_keys, base_rows)
    source = jnp.take_along_axis(source_perm, jnp.broadcast_to(image_pos % dp_count, (sections, GROUP_IMAGES)), axis=1)
    position = source * IMG_DEV + image_pos[None, :] // dp_count
    section_rows = jnp.broadcast_to(section_ids[:, None], (sections, GROUP_IMAGES))
    route = jnp.zeros((sections, GROUP_IMAGES), jnp.int32).at[section_rows, position].set(codes)
    return (shuffled.reshape(SEQS), route.reshape(IMAGES))


def draw_image_counts(key, part):
    return counts_and_route(key)[0]


def draw_image_route(key, part):
    return counts_and_route(key)[1]


def draw_text_lengths(key, part):
    lengths = jax.random.randint(key, (SEQS,), 1, LEN + 1)
    return lengths.at[::SEQ_DEV].set(LEN).astype(jnp.int32)


def gain_values(key):
    return jnp.exp(jax.random.uniform(key, (HD,), jnp.float32, math.log(0.6), math.log(1.7)))


def draw_q_gain(key, part):
    return gain_values(jax.random.fold_in(key, 21))


def draw_k_gain(key, part):
    return gain_values(jax.random.fold_in(key, 22))


def draw_queries(key, part):
    noise = jax.random.normal(jax.random.fold_in(key, 32), (SEQS, LEN, KVH, GROUP, HD), jnp.float32)
    mixed = noise
    return jnp.clip(mixed, -6.0, 6.0).reshape(TOKENS, H * HD).astype(jnp.bfloat16)


def draw_keys_raw(key, part):
    noise = jax.random.normal(jax.random.fold_in(key, 33), (IMAGES, PATCH, KVH, HD), jnp.float32)
    mixed = noise
    return jnp.clip(mixed, -6.0, 6.0).reshape(IMAGES, PATCH, KVH * HD).astype(jnp.bfloat16)


def shard_levels(stream_key, dims, pieces, low, high):
    def one(dim, blocks):
        draws = jax.random.uniform(jax.random.fold_in(jax.random.fold_in(stream_key, 6), dim), (blocks,), jnp.float32, low / len(pieces), high / len(pieces))
        return jnp.repeat(jnp.exp(draws), dims[dim] // blocks).reshape((-1,) + (1,) * (len(dims) - dim - 1))

    level = one(*pieces[0])
    for cut in pieces[1:]:
        level = level * one(*cut)
    return level


def normal_values(key, extent, deviation, bound, shards=(), held_as=jnp.bfloat16):
    drawn = deviation * jax.random.normal(key, extent, jnp.float32)
    if shards:
        drawn = drawn * shard_levels(key, extent, shards, -0.22, 0.18)
    return jnp.clip(drawn, -bound, bound).astype(held_as)


def setup_inputs(seed: int = 0) -> dict:
    splits = jax.random.split(jax.random.key(seed), 10)
    return {
        "queries": draw_queries(jax.random.fold_in(splits[9], 71), 0),
        "cotangent": normal_values(splits[1], (TOKENS, H * HD), 1.0, 6.0, ((0, 8), (1, 4))),
        "keys_raw": draw_keys_raw(jax.random.fold_in(splits[9], 71), 0),
        "values": normal_values(splits[3], (IMAGES, PATCH, KVH * HD), 1.0, 6.0, ((0, 8), (2, 4))),
        "image_counts": draw_image_counts(jax.random.fold_in(splits[9], 71), 0),
        "image_route": draw_image_route(jax.random.fold_in(splits[9], 71), 0),
        "text_lengths": draw_text_lengths(jax.random.fold_in(splits[9], 71), 0),
        "q_gain": draw_q_gain(jax.random.fold_in(splits[9], 71), 0),
        "k_gain": draw_k_gain(jax.random.fold_in(splits[9], 71), 0),
    }


def norm_forward(inputs, norm_gain):
    wide = inputs.astype(jnp.float32)
    inv_rms = lax.rsqrt(lax.optimization_barrier(jnp.mean(wide * wide, axis=-1, keepdims=True)) + 1e-05)
    return (wide * inv_rms * norm_gain).astype(jnp.bfloat16)

def norm_backward(inputs, norm_gain, upstream):
    wide = inputs.astype(jnp.float32)
    inv_rms = lax.rsqrt(lax.optimization_barrier(jnp.mean(wide * wide, axis=-1, keepdims=True)) + 1e-05)
    scaled = norm_gain * upstream
    grad_in = inv_rms * scaled - wide * inv_rms ** 3 * lax.optimization_barrier(jnp.mean(wide * scaled, axis=-1, keepdims=True))
    gain_grad = lax.optimization_barrier(jnp.sum((upstream * wide * inv_rms).reshape(-1, inputs.shape[-1]), axis=0))
    return (grad_in.astype(jnp.bfloat16), gain_grad)

def attend(query_norm, slot_keys, slot_vals, live_keys, grad):
    scaling = HD ** (-0.5)
    qwide = query_norm.astype(jnp.float32)
    kwide = slot_keys.astype(jnp.float32)
    vwide = slot_vals.astype(jnp.float32)
    gwide = grad.astype(jnp.float32)
    scores = jnp.einsum('slkgd,sjkd->skglj', qwide, kwide) * scaling
    scores = jnp.where(live_keys[:, None, None, None, :], scores, -1e+30)
    row_top = lax.optimization_barrier(jnp.max(scores, axis=-1, keepdims=True))
    expo = jnp.exp(scores - row_top)
    probs = expo / lax.optimization_barrier(jnp.sum(expo, axis=-1, keepdims=True))
    probs_low = probs.astype(jnp.bfloat16)
    pwide = probs_low.astype(jnp.float32)
    output = jnp.einsum('skglj,sjkd->slkgd', pwide, vwide)
    dprob = jnp.einsum('slkgd,sjkd->skglj', gwide, vwide)
    row_dots = jnp.transpose(lax.optimization_barrier(jnp.sum(gwide * output, axis=-1)), (0, 2, 3, 1))
    dscore = (probs * (dprob - row_dots[..., None])).astype(jnp.bfloat16)
    dwide = dscore.astype(jnp.float32)
    dq_norm = jnp.einsum('skglj,sjkd->slkgd', dwide, kwide) * scaling
    dk_slots = (jnp.einsum('skglj,slkgd->sjkd', dwide, qwide) * scaling).astype(jnp.bfloat16)
    dv_slots = jnp.einsum('skglj,slkgd->sjkd', pwide, gwide).astype(jnp.bfloat16)
    return (dq_norm, dk_slots, dv_slots)

def reference(queries, cotangent, keys_raw, values, image_counts, image_route, text_lengths, q_gain, k_gain):
    raw_heads = keys_raw.reshape(IMAGES, PATCH, KVH, HD)
    key_norm = norm_forward(raw_heads, k_gain)
    slot_keys = jnp.zeros((SEQS * 4, PATCH, KVH, HD), jnp.bfloat16).at[image_route].set(key_norm)
    slot_vals = jnp.zeros((SEQS * 4, PATCH, KVH, HD), jnp.bfloat16).at[image_route].set(values.reshape(IMAGES, PATCH, KVH, HD))
    slot_keys = slot_keys.reshape(SEQS, 4 * PATCH, KVH, HD)
    slot_vals = slot_vals.reshape(SEQS, 4 * PATCH, KVH, HD)
    q_heads = queries.reshape(SEQS, LEN, KVH, GROUP, HD)
    query_norm = norm_forward(q_heads, q_gain)
    live_rows = jnp.arange(LEN)[None, :] < text_lengths[:, None]
    grad = jnp.where(live_rows[:, :, None, None, None], cotangent.reshape(SEQS, LEN, KVH, GROUP, HD), 0).astype(jnp.bfloat16)
    live_keys = (jnp.arange(4 * PATCH) // PATCH)[None, :] < image_counts[:, None]
    blocks = SEQS // SEQ_DEV

    def split_blocks(array):
        return array.reshape((blocks, SEQ_DEV) + array.shape[1:])

    def one_block(items):
        return attend(items[0], items[1], items[2], items[3], items[4])
    dq_norm, dk_slots, dv_slots = lax.map(one_block, (split_blocks(query_norm), split_blocks(slot_keys), split_blocks(slot_vals), split_blocks(live_keys), split_blocks(grad)))
    dq_norm = dq_norm.reshape(SEQS, LEN, KVH, GROUP, HD)
    dk_norm = dk_slots.reshape(SEQS * 4, PATCH, KVH, HD)[image_route]
    value_grad = dv_slots.reshape(SEQS * 4, PATCH, KVH, HD)[image_route]
    query_grad, q_gain_grad = norm_backward(q_heads, q_gain, dq_norm)
    key_grad, k_gain_grad = norm_backward(raw_heads, k_gain, dk_norm.astype(jnp.float32))
    return (query_grad.reshape(TOKENS, H * HD), key_grad.reshape(IMAGES, PATCH, KVH * HD), value_grad.reshape(IMAGES, PATCH, KVH * HD), q_gain_grad, k_gain_grad)
```

```python
import functools

import jax
import jax.numpy as jnp
from jax import lax
from jax.experimental import pallas as pl
from jax.experimental.pallas import tpu as pltpu
from jax.sharding import PartitionSpec as P

MESH = pl.DeviceIdType.MESH
AXES = ("mp", "dp", "sec")
F32 = jnp.float32
BF16 = jnp.bfloat16


def dot(a, b, ca, cb):
    return lax.dot_general(a, b, (((ca,), (cb,)), ((), ())), preferred_element_type=F32)


def fold_rows(x):
    return jnp.sum(x.reshape(x.shape[0] // 8, 8, x.shape[1]), axis=0)


def fused(
    dims,
    q_hbm,
    c_hbm,
    k_hbm,
    v_hbm,
    counts,
    route,
    lens,
    q_gain,
    k_gain,
    dq_hbm,
    dk_hbm,
    dv_hbm,
    gq_out,
    gk_out,
    bufs,
    sends,
    recvs,
    grads,
    backs,
    homes,
    parts,
    gathers,
    sems,
    gain_sems,
):
    seq_dev, seq_len, img_dev, patches, heads, group, hd, cap, sizes = dims
    (q_v, c_v, own_k, own_v, xhat_v, rinv_v, qn_v, gr_v, dq_v, dk_v, dv_v) = bufs[:11]
    (acc, route_out, route_in, route_s, slot_own, slot_cell, slot_flag, cell_slot,
     home_slot, home_cell, home_flag) = bufs[11:]
    (in_sem, out_sem, rt_send, rt_recv, rt_local, kv_send, kv_recv, bk_send, bk_recv) = sems
    dp = sizes["dp"]
    me = lax.axis_index("dp")
    scaling = hd ** (-0.5)
    slots = 4 * seq_dev
    first_code = (lax.axis_index("sec") * dp + me) * slots

    def peer(axis, offset):
        return lax.rem(lax.axis_index(axis) + offset, sizes[axis])

    barrier = pltpu.get_barrier_semaphore()
    for axis in AXES:
        for o in range(1, sizes[axis]):
            pl.semaphore_signal(barrier, inc=1, device_id={axis: peer(axis, o)}, device_id_type=MESH)

    in_copies = [
        pltpu.make_async_copy(src, dst, in_sem.at[n])
        for n, (src, dst) in enumerate(((k_hbm, own_k), (v_hbm, own_v), (q_hbm, q_v), (c_hbm, c_v)))
    ]
    for copy in in_copies:
        copy.start()

    lane = lax.broadcasted_iota(jnp.int32, (1, 128), 1)
    codes = [route[i] for i in range(img_dev)]
    packed = jnp.zeros((1, 128), jnp.int32)
    for i in range(img_dev):
        packed = jnp.where(lane == i, codes[i], packed)
    route_out[...] = packed
    target = [lax.rem(lax.div(codes[i], slots), dp) for i in range(img_dev)]

    for i in range(img_dev):
        order = jnp.int32(0)
        for j in range(i):
            order = order + jnp.where(target[j] == target[i], 1, 0)
        mine = target[i] == me
        home_flag[i] = jnp.where(mine, 1, 0)
        home_slot[i] = jnp.where(mine, jnp.clip(codes[i] - first_code, 0, slots - 1), 0)
        home_cell[i] = jnp.where(mine, peer("dp", 1) * cap, target[i] * cap + jnp.minimum(order, cap - 1))

    def send_cells(h, d):
        for c in range(cap):
            image = jnp.int32(0)
            for i in range(img_dev):
                image = jnp.where(home_cell[i] == d * cap + c, jnp.where(target[i] == d, i, image), image)
            sends[h][d, c, 0] = own_k[image, :, h * hd : (h + 1) * hd]
            sends[h][d, c, 1] = own_v[image, :, h * hd : (h + 1) * hd]

    def kv_copy(h, d, slot):
        return pltpu.make_async_remote_copy(
            src_ref=sends[h].at[d],
            dst_ref=recvs[h].at[slot],
            send_sem=kv_send.at[h, d],
            recv_sem=kv_recv.at[h, slot],
            device_id={"dp": d},
            device_id_type=MESH,
        )

    def back_copy(h, d, slot):
        return pltpu.make_async_remote_copy(
            src_ref=backs[h].at[d],
            dst_ref=homes[h].at[slot],
            send_sem=bk_send.at[h, d],
            recv_sem=bk_recv.at[h, slot],
            device_id={"dp": d},
            device_id_type=MESH,
        )

    def route_copy(d, slot):
        return pltpu.make_async_remote_copy(
            src_ref=route_out,
            dst_ref=route_in.at[slot],
            send_sem=rt_send.at[d],
            recv_sem=rt_recv.at[slot],
            device_id={"dp": d},
            device_id_type=MESH,
        )

    def peers(body):
        if dp == 2:
            body(peer("dp", 1))
        else:

            def step(o, carry):
                body(peer("dp", o))
                return carry

            lax.fori_loop(1, dp, step, 0)

    in_copies[0].wait()
    in_copies[1].wait()
    peers(lambda d: send_cells(0, d))
    pl.semaphore_wait(barrier, sum(sizes[a] - 1 for a in AXES))
    peers(lambda d: route_copy(d, me).start())
    peers(lambda d: kv_copy(0, d, me).start())
    for h in range(1, heads):
        peers(lambda d: send_cells(h, d))
        peers(lambda d: kv_copy(h, d, me).start())

    in_copies[2].wait()
    in_copies[3].wait()
    qg = q_gain[...]
    kg = k_gain[...]
    rows = group * seq_len
    row_token = lax.rem(lax.broadcasted_iota(jnp.int32, (rows, 1), 0), seq_len)

    def stack(ref, s, h):
        return jnp.concatenate(
            [
                ref[pl.ds(pl.multiple_of(s * seq_len, seq_len), seq_len), (h * group + g) * hd : (h * group + g + 1) * hd]
                for g in range(group)
            ],
            axis=0,
        )

    def prepare(s, carry):
        for h in range(heads):
            x = stack(q_v, s, h).astype(F32)
            r = lax.rsqrt(jnp.mean(x * x, axis=-1, keepdims=True) + 1e-05)
            xr = x * r
            xhat_v[h, s] = xr
            rinv_v[h, s] = jnp.broadcast_to(r, xr.shape)
            qn_v[h, s] = (xr * qg).astype(BF16)
            grad = stack(c_v, s, h)
            gr_v[h, s] = jnp.where(row_token < lens[s], grad, jnp.zeros_like(grad))
        return carry

    lax.fori_loop(0, seq_dev, prepare, 0)
    acc[...] = jnp.zeros_like(acc)

    for q in range(slots):
        own = jnp.int32(0)
        flag = jnp.int32(0)
        for i in range(img_dev):
            match = codes[i] - first_code == q
            own = jnp.where(match, i, own)
            flag = jnp.where(match, 1, flag)
        slot_own[q] = own
        slot_flag[q] = flag
        slot_cell[q] = peer("dp", 1) * cap

    peers(lambda d: route_copy(d, d).wait_recv())
    peers(lambda d: pltpu.make_async_copy(route_in.at[d], route_s.at[d], rt_local.at[d]).start())
    peers(lambda d: pltpu.make_async_copy(route_in.at[d], route_s.at[d], rt_local.at[d]).wait())

    def scan_source(d):
        run = jnp.int32(0)
        local, place = [], []
        for i in range(img_dev):
            code = route_s[d, 0, i] - first_code
            mine = (code >= 0) & (code < slots)
            local.append(jnp.where(mine, code, -1))
            place.append(jnp.where(mine, jnp.minimum(run, cap - 1), -1))
            run = run + jnp.where(mine, 1, 0)
        for q in range(slots):
            cell = slot_cell[q]
            for i in range(img_dev):
                cell = jnp.where(local[i] == q, d * cap + place[i], cell)
            slot_cell[q] = cell
        for c in range(cap):
            slot = jnp.int32(0)
            for i in range(img_dev):
                slot = jnp.where(place[i] == c, local[i], slot)
            cell_slot[d * cap + c] = slot

    peers(scan_source)

    keys = 4 * patches
    col_image = lax.div(lax.broadcasted_iota(jnp.int32, (1, keys), 1), patches)

    def attend(h, s):
        raw, val = [], []
        for p in range(4):
            n = 4 * s + p
            own, cell = slot_own[n], slot_cell[n]
            mine = slot_flag[n] == 1
            live = p < counts[s]
            cd, cc = lax.div(cell, cap), lax.rem(cell, cap)
            k_one = jnp.where(mine, own_k[own, :, h * hd : (h + 1) * hd], recvs[h][cd, cc, 0])
            v_one = jnp.where(mine, own_v[own, :, h * hd : (h + 1) * hd], recvs[h][cd, cc, 1])
            raw.append(jnp.where(live, k_one, jnp.zeros_like(k_one)))
            val.append(jnp.where(live, v_one, jnp.zeros_like(v_one)))
        kx = jnp.concatenate(raw, axis=0).astype(F32)
        v = jnp.concatenate(val, axis=0)
        kx = kx * lax.rsqrt(jnp.mean(kx * kx, axis=-1, keepdims=True) + 1e-05)
        kn = (kx * kg).astype(BF16)
        qn = qn_v[h, s]
        grad = gr_v[h, s]
        scores = jnp.where(col_image < counts[s], dot(qn, kn, 1, 1) * scaling, -1e30)
        dprob = dot(grad, v, 1, 1)
        expo = jnp.exp(scores - jnp.max(scores, axis=-1, keepdims=True))
        probs = expo * (1.0 / jnp.sum(expo, axis=-1, keepdims=True))
        low = probs.astype(BF16)
        row_dots = jnp.sum(low.astype(F32) * dprob, axis=-1, keepdims=True)
        dscore = (probs * (dprob - row_dots)).astype(BF16)
        dv = dot(low, grad, 0, 0).astype(BF16)
        dk = (dot(dscore, qn, 0, 0) * scaling).astype(BF16)
        dq = dot(dscore, kn, 1, 0) * scaling
        for p in range(4):
            grads[h][4 * s + p, 0] = dk[p * patches : (p + 1) * patches]
            grads[h][4 * s + p, 1] = dv[p * patches : (p + 1) * patches]
        acc[1] += fold_rows(dk.astype(F32) * kx)
        xr = xhat_v[h, s]
        prod = xr * dq
        acc[0] += fold_rows(prod)
        mean = jnp.mean(prod * qg, axis=-1, keepdims=True)
        dx = (rinv_v[h, s] * (dq * qg - xr * mean)).astype(BF16)
        for g in range(group):
            dq_v[
                pl.ds(pl.multiple_of(s * seq_len, seq_len), seq_len),
                (h * group + g) * hd : (h * group + g + 1) * hd,
            ] = dx[g * seq_len : (g + 1) * seq_len]

    def fill_back(h, d):
        for c in range(cap):
            slot = cell_slot[d * cap + c]
            backs[h][d, c] = grads[h][slot]

    out_copies = []
    width = group * hd
    for h in range(heads):
        peers(lambda d: kv_copy(h, d, d).wait_recv())

        def seq_step(s, carry):
            attend(h, s)
            return carry

        lax.fori_loop(0, seq_dev, seq_step, 0)
        peers(lambda d: fill_back(h, d))
        peers(lambda d: back_copy(h, d, me).start())
        copy = pltpu.make_async_copy(
            dq_v.at[:, h * width : (h + 1) * width], dq_hbm.at[:, h * width : (h + 1) * width], out_sem.at[h]
        )
        copy.start()
        out_copies.append(copy)

    def gain_copy(n, o, slot):
        axis = AXES[n]
        return pltpu.make_async_remote_copy(
            src_ref=parts.at[n],
            dst_ref=gathers[n].at[slot],
            send_sem=gain_sems[2 * n].at[o],
            recv_sem=gain_sems[2 * n + 1].at[slot],
            device_id={axis: peer(axis, o)},
            device_id_type=MESH,
        )

    def gain_send(n, value):
        mine = lax.axis_index(AXES[n])
        parts[n] = value
        gathers[n][mine] = value
        for o in range(1, sizes[AXES[n]]):
            gain_copy(n, o, mine).start()

    def gain_recv(n):
        for o in range(1, sizes[AXES[n]]):
            gain_copy(n, o, peer(AXES[n], o)).wait_recv()
        total = gathers[n][0]
        for j in range(1, sizes[AXES[n]]):
            total = total + gathers[n][j]
        return total

    def finish(h):
        peers(lambda d: back_copy(h, d, d).wait_recv())
        for i in range(img_dev):
            cell = home_cell[i]
            cd, cc = lax.div(cell, cap), lax.rem(cell, cap)
            both = jnp.where(home_flag[i] == 1, grads[h][home_slot[i]], homes[h][cd, cc])
            dv_v[i, :, h * hd : (h + 1) * hd] = both[1]
            dy = both[0].astype(F32)
            x = own_k[i, :, h * hd : (h + 1) * hd].astype(F32)
            r = lax.rsqrt(jnp.mean(x * x, axis=-1, keepdims=True) + 1e-05)
            u = kg * dy
            xr = x * r
            dk_v[i, :, h * hd : (h + 1) * hd] = (
                r * (u - xr * jnp.mean(xr * u, axis=-1, keepdims=True))
            ).astype(BF16)

    gain_send(0, jnp.sum(acc[...], axis=1))
    for h in range(heads - 1):
        finish(h)
    gain_send(1, gain_recv(0))
    gain_send(2, gain_recv(1))
    finish(heads - 1)
    for n, (src, dst) in enumerate(((dk_v, dk_hbm), (dv_v, dv_hbm))):
        copy = pltpu.make_async_copy(src, dst, out_sem.at[heads + n])
        copy.start()
        out_copies.append(copy)
    total = gain_recv(2)
    gq_out[...] = total[0:1]
    gk_out[...] = total[1:2]

    for copy in out_copies:
        copy.wait()
    peers(lambda d: route_copy(d, me).wait_send())
    for h in range(heads):
        peers(lambda d: kv_copy(h, d, me).wait_send())
        peers(lambda d: back_copy(h, d, me).wait_send())
    for n in range(len(AXES)):
        for o in range(1, sizes[AXES[n]]):
            gain_copy(n, o, lax.axis_index(AXES[n])).wait_send()


def on_device(
    queries, cotangent, keys_raw, values, image_counts, image_route, text_lengths, q_gain, k_gain
):
    sizes = {axis: lax.axis_size(axis) for axis in AXES}
    dp = sizes["dp"]
    seq_dev = image_counts.shape[0]
    img_dev, patches, kv_width = keys_raw.shape
    hd = q_gain.shape[0]
    heads = kv_width // hd
    tokens = queries.shape[0]
    seq_len = tokens // seq_dev
    group = queries.shape[1] // hd // heads
    cap = (4 * seq_dev + dp - 1) // dp
    slots = 4 * seq_dev
    rows = group * seq_len
    dims = (seq_dev, seq_len, img_dev, patches, heads, group, hd, cap, sizes)
    cells = (dp, cap, 2, patches, hd)
    vmem, smem, dma = pltpu.VMEM, pltpu.SMEM, pltpu.SemaphoreType.DMA
    unit = (heads, seq_dev, rows, hd)
    scratch = [
        [
            vmem(queries.shape, BF16),
            vmem(queries.shape, BF16),
            vmem(keys_raw.shape, BF16),
            vmem(keys_raw.shape, BF16),
            vmem(unit, F32),
            vmem(unit, F32),
            vmem(unit, BF16),
            vmem(unit, BF16),
            vmem(queries.shape, BF16),
            vmem(keys_raw.shape, BF16),
            vmem(keys_raw.shape, BF16),
            vmem((2, 8, hd), F32),
            vmem((1, 128), jnp.int32),
            vmem((dp, 1, 128), jnp.int32),
            smem((dp, 1, 128), jnp.int32),
            smem((slots,), jnp.int32),
            smem((slots,), jnp.int32),
            smem((slots,), jnp.int32),
            smem((dp * cap,), jnp.int32),
            smem((img_dev,), jnp.int32),
            smem((img_dev,), jnp.int32),
            smem((img_dev,), jnp.int32),
        ],
        [vmem(cells, BF16) for _ in range(heads)],
        [vmem(cells, BF16) for _ in range(heads)],
        [vmem((slots, 2, patches, hd), BF16) for _ in range(heads)],
        [vmem(cells, BF16) for _ in range(heads)],
        [vmem(cells, BF16) for _ in range(heads)],
        vmem((len(AXES), 2, hd), F32),
        [vmem((sizes[a], 2, hd), F32) for a in AXES],
        [
            dma((4,)),
            dma((heads + 2,)),
            dma((dp,)),
            dma((dp,)),
            dma((dp,)),
            dma((heads, dp)),
            dma((heads, dp)),
            dma((heads, dp)),
            dma((heads, dp)),
        ],
        [dma((sizes[a],)) for a in AXES for _ in range(2)],
    ]
    hbm = pl.BlockSpec(memory_space=pl.ANY)
    in_smem = pl.BlockSpec(memory_space=pltpu.SMEM)
    in_vmem = pl.BlockSpec(memory_space=pltpu.VMEM)
    query_grad, key_grad, value_grad, gq, gk = pl.pallas_call(
        functools.partial(fused, dims),
        out_shape=(
            jax.ShapeDtypeStruct(queries.shape, BF16),
            jax.ShapeDtypeStruct(keys_raw.shape, BF16),
            jax.ShapeDtypeStruct(values.shape, BF16),
            jax.ShapeDtypeStruct((1, hd), F32),
            jax.ShapeDtypeStruct((1, hd), F32),
        ),
        in_specs=[hbm] * 4 + [in_smem] * 3 + [in_vmem] * 2,
        out_specs=(hbm, hbm, hbm, in_vmem, in_vmem),
        scratch_shapes=scratch,
        compiler_params=pltpu.CompilerParams(collective_id=0, has_side_effects=True),
        name="relay_attention",
    )(
        queries,
        cotangent,
        keys_raw,
        values,
        image_counts,
        image_route,
        text_lengths,
        q_gain.reshape(1, hd),
        k_gain.reshape(1, hd),
    )
    return (query_grad, key_grad, value_grad, gq.reshape(hd), gk.reshape(hd))


def solution(mesh):
    placed = (
        P(("sec", "dp"), "mp"),
        P(("sec", "dp"), "mp"),
        P(("sec", "dp"), None, "mp"),
        P(("sec", "dp"), None, "mp"),
        P(("sec", "dp")),
        P(("sec", "dp")),
        P(("sec", "dp")),
        P(),
        P(),
    )
    return jax.shard_map(
        on_device,
        mesh=mesh,
        in_specs=placed,
        out_specs=(
            P(("sec", "dp"), "mp"),
            P(("sec", "dp"), None, "mp"),
            P(("sec", "dp"), None, "mp"),
            P(),
            P(),
        ),
        check_vma=False,
    )
```

```python
import functools

import jax
import jax.numpy as jnp
from jax import lax
from jax.experimental import pallas as pl
from jax.experimental.pallas import tpu as pltpu
from jax.sharding import PartitionSpec as P

MESH = pl.DeviceIdType.MESH
AXES = ("dp", "mp", "sec")
F32 = jnp.float32
BF16 = jnp.bfloat16


def dot(a, b, ca, cb):
    return lax.dot_general(a, b, (((ca,), (cb,)), ((), ())), preferred_element_type=F32)


def fold_rows(x):
    return jnp.sum(x.reshape(x.shape[0] // 8, 8, x.shape[1]), axis=0)


def fused(
    dims,
    q_hbm,
    c_hbm,
    k_hbm,
    v_hbm,
    counts_hbm,
    route_hbm,
    lens_hbm,
    q_gain_hbm,
    k_gain_hbm,
    dq_v,
    dk_v,
    dv_v,
    gq_out,
    gk_out,
    bufs,
    sends,
    recvs,
    grads,
    backs,
    homes,
    parts,
    gathers,
    sems,
    gain_sems,
):
    seq_dev, seq_len, img_dev, patches, heads, group, hd, cap, sizes = dims
    (q_v, c_v, own_k, own_v, xhat_v, rinv_v, qn_v, gr_v, counts, route, lens) = bufs[:11]
    q_gain, k_gain = bufs[22:]
    (acc, route_out, route_in, route_s, slot_own, slot_cell, slot_flag, cell_slot,
     home_slot, home_cell, home_flag) = bufs[11:22]
    (in_sem, rt_send, rt_recv, rt_local, kv_send, kv_recv, bk_send, bk_recv) = sems
    dp = sizes["dp"]
    me = lax.axis_index("dp")
    scaling = hd ** (-0.5)
    slots = 4 * seq_dev
    first_code = (lax.axis_index("sec") * dp + me) * slots

    def peer(axis, offset):
        return lax.rem(lax.axis_index(axis) + offset, sizes[axis])

    barrier = pltpu.get_barrier_semaphore()
    for axis in AXES:
        for o in range(1, sizes[axis]):
            pl.semaphore_signal(barrier, inc=1, device_id={axis: peer(axis, o)}, device_id_type=MESH)

    in_copies = [
        pltpu.make_async_copy(src, dst, in_sem.at[n])
        for n, (src, dst) in enumerate(
            (
                (route_hbm, route),
                (k_hbm, own_k),
                (v_hbm, own_v),
                (q_hbm, q_v),
                (c_hbm, c_v),
                (counts_hbm, counts),
                (lens_hbm, lens),
                (q_gain_hbm, q_gain),
                (k_gain_hbm, k_gain),
            )
        )
    ]
    for copy in in_copies:
        copy.start()

    lane = lax.broadcasted_iota(jnp.int32, (1, 128), 1)
    in_copies[0].wait()
    codes = [route[i] for i in range(img_dev)]
    packed = jnp.zeros((1, 128), jnp.int32)
    for i in range(img_dev):
        packed = jnp.where(lane == i, codes[i], packed)
    route_out[...] = packed
    target = [lax.rem(lax.div(codes[i], slots), dp) for i in range(img_dev)]

    for i in range(img_dev):
        order = jnp.int32(0)
        for j in range(i):
            order = order + jnp.where(target[j] == target[i], 1, 0)
        mine = target[i] == me
        home_flag[i] = jnp.where(mine, 1, 0)
        home_slot[i] = jnp.where(mine, jnp.clip(codes[i] - first_code, 0, slots - 1), 0)
        home_cell[i] = jnp.where(mine, peer("dp", 1) * cap, target[i] * cap + jnp.minimum(order, cap - 1))

    def send_cells(h, d):
        for c in range(cap):
            image = jnp.int32(0)
            for i in range(img_dev):
                image = jnp.where(home_cell[i] == d * cap + c, jnp.where(target[i] == d, i, image), image)
            sends[h][d, c, 0] = own_k[image, :, h * hd : (h + 1) * hd]
            sends[h][d, c, 1] = own_v[image, :, h * hd : (h + 1) * hd]

    def kv_copy(h, d, slot):
        return pltpu.make_async_remote_copy(
            src_ref=sends[h].at[d],
            dst_ref=recvs[h].at[slot],
            send_sem=kv_send.at[h, d],
            recv_sem=kv_recv.at[h, slot],
            device_id={"dp": d},
            device_id_type=MESH,
        )

    def back_copy(h, d, slot):
        return pltpu.make_async_remote_copy(
            src_ref=backs[h].at[d],
            dst_ref=homes[h].at[slot],
            send_sem=bk_send.at[h, d],
            recv_sem=bk_recv.at[h, slot],
            device_id={"dp": d},
            device_id_type=MESH,
        )

    def route_copy(d, slot):
        return pltpu.make_async_remote_copy(
            src_ref=route_out,
            dst_ref=route_in.at[slot],
            send_sem=rt_send.at[d],
            recv_sem=rt_recv.at[slot],
            device_id={"dp": d},
            device_id_type=MESH,
        )

    def peers(body):
        if dp == 2:
            body(peer("dp", 1))
        else:

            def step(o, carry):
                body(peer("dp", o))
                return carry

            lax.fori_loop(1, dp, step, 0)

    in_copies[1].wait()
    in_copies[2].wait()
    peers(lambda d: send_cells(0, d))
    pl.semaphore_wait(barrier, sum(sizes[a] - 1 for a in AXES))
    peers(lambda d: route_copy(d, me).start())
    peers(lambda d: kv_copy(0, d, me).start())
    for h in range(1, heads):
        peers(lambda d: send_cells(h, d))
        peers(lambda d: kv_copy(h, d, me).start())

    for copy in in_copies[3:]:
        copy.wait()
    qg = q_gain[...]
    kg = k_gain[...]
    rows = group * seq_len
    row_token = lax.rem(lax.broadcasted_iota(jnp.int32, (rows, 1), 0), seq_len)

    def stack(ref, s, h):
        return jnp.concatenate(
            [
                ref[pl.ds(pl.multiple_of(s * seq_len, seq_len), seq_len), (h * group + g) * hd : (h * group + g + 1) * hd]
                for g in range(group)
            ],
            axis=0,
        )

    def prepare(s, carry):
        for h in range(heads):
            x = stack(q_v, s, h).astype(F32)
            r = lax.rsqrt(jnp.mean(x * x, axis=-1, keepdims=True) + 1e-05)
            xr = x * r
            xhat_v[h, s] = xr
            rinv_v[h, s] = jnp.broadcast_to(r, xr.shape)
            qn_v[h, s] = (xr * qg).astype(BF16)
            grad = stack(c_v, s, h)
            gr_v[h, s] = jnp.where(row_token < lens[s], grad, jnp.zeros_like(grad))
        return carry

    lax.fori_loop(0, seq_dev, prepare, 0)
    acc[...] = jnp.zeros_like(acc)

    for q in range(slots):
        own = jnp.int32(0)
        flag = jnp.int32(0)
        for i in range(img_dev):
            match = codes[i] - first_code == q
            own = jnp.where(match, i, own)
            flag = jnp.where(match, 1, flag)
        slot_own[q] = own
        slot_flag[q] = flag
        slot_cell[q] = peer("dp", 1) * cap

    peers(lambda d: route_copy(d, d).wait_recv())
    peers(lambda d: pltpu.make_async_copy(route_in.at[d], route_s.at[d], rt_local.at[d]).start())
    peers(lambda d: pltpu.make_async_copy(route_in.at[d], route_s.at[d], rt_local.at[d]).wait())

    def scan_source(d):
        run = jnp.int32(0)
        local, place = [], []
        for i in range(img_dev):
            code = route_s[d, 0, i] - first_code
            mine = (code >= 0) & (code < slots)
            local.append(jnp.where(mine, code, -1))
            place.append(jnp.where(mine, jnp.minimum(run, cap - 1), -1))
            run = run + jnp.where(mine, 1, 0)
        for q in range(slots):
            cell = slot_cell[q]
            for i in range(img_dev):
                cell = jnp.where(local[i] == q, d * cap + place[i], cell)
            slot_cell[q] = cell
        for c in range(cap):
            slot = jnp.int32(0)
            for i in range(img_dev):
                slot = jnp.where(place[i] == c, local[i], slot)
            cell_slot[d * cap + c] = slot

    peers(scan_source)

    keys = 4 * patches
    col_image = lax.div(lax.broadcasted_iota(jnp.int32, (1, keys), 1), patches)

    def attend(h, s):
        raw, val = [], []
        for p in range(4):
            n = 4 * s + p
            own, cell = slot_own[n], slot_cell[n]
            mine = slot_flag[n] == 1
            live = p < counts[s]
            cd, cc = lax.div(cell, cap), lax.rem(cell, cap)
            k_one = jnp.where(mine, own_k[own, :, h * hd : (h + 1) * hd], recvs[h][cd, cc, 0])
            v_one = jnp.where(mine, own_v[own, :, h * hd : (h + 1) * hd], recvs[h][cd, cc, 1])
            raw.append(jnp.where(live, k_one, jnp.zeros_like(k_one)))
            val.append(jnp.where(live, v_one, jnp.zeros_like(v_one)))
        kx = jnp.concatenate(raw, axis=0).astype(F32)
        v = jnp.concatenate(val, axis=0)
        kx = kx * lax.rsqrt(jnp.mean(kx * kx, axis=-1, keepdims=True) + 1e-05)
        kn = (kx * kg).astype(BF16)
        qn = qn_v[h, s]
        grad = gr_v[h, s]
        scores = jnp.where(col_image < counts[s], dot(qn, kn, 1, 1) * scaling, -1e30)
        dprob = dot(grad, v, 1, 1)
        expo = jnp.exp(scores - jnp.max(scores, axis=-1, keepdims=True))
        probs = expo * (1.0 / jnp.sum(expo, axis=-1, keepdims=True))
        low = probs.astype(BF16)
        row_dots = jnp.sum(low.astype(F32) * dprob, axis=-1, keepdims=True)
        dscore = (probs * (dprob - row_dots)).astype(BF16)
        dv = dot(low, grad, 0, 0).astype(BF16)
        dk = (dot(dscore, qn, 0, 0) * scaling).astype(BF16)
        dq = dot(dscore, kn, 1, 0) * scaling
        for p in range(4):
            grads[h][4 * s + p, 0] = dk[p * patches : (p + 1) * patches]
            grads[h][4 * s + p, 1] = dv[p * patches : (p + 1) * patches]
        acc[1] += fold_rows(dk.astype(F32) * kx)
        xr = xhat_v[h, s]
        prod = xr * dq
        acc[0] += fold_rows(prod)
        mean = jnp.mean(prod * qg, axis=-1, keepdims=True)
        dx = (rinv_v[h, s] * (dq * qg - xr * mean)).astype(BF16)
        for g in range(group):
            dq_v[
                pl.ds(pl.multiple_of(s * seq_len, seq_len), seq_len),
                (h * group + g) * hd : (h * group + g + 1) * hd,
            ] = dx[g * seq_len : (g + 1) * seq_len]

    def fill_back(h, d):
        for c in range(cap):
            slot = cell_slot[d * cap + c]
            backs[h][d, c] = grads[h][slot]

    def gain_copy(n, o, slot):
        axis = AXES[n]
        return pltpu.make_async_remote_copy(
            src_ref=parts.at[n],
            dst_ref=gathers[n].at[slot],
            send_sem=gain_sems[2 * n].at[o],
            recv_sem=gain_sems[2 * n + 1].at[slot],
            device_id={axis: peer(axis, o)},
            device_id_type=MESH,
        )

    def gain_send(n, value):
        mine = lax.axis_index(AXES[n])
        parts[n] = value
        gathers[n][mine] = value
        for o in range(1, sizes[AXES[n]]):
            gain_copy(n, o, mine).start()

    def gain_recv(n):
        for o in range(1, sizes[AXES[n]]):
            gain_copy(n, o, peer(AXES[n], o)).wait_recv()
        total = gathers[n][0]
        for j in range(1, sizes[AXES[n]]):
            total = total + gathers[n][j]
        return total

    for h in range(heads):
        peers(lambda d: kv_copy(h, d, d).wait_recv())

        def seq_step(s, carry):
            attend(h, s)
            return carry

        lax.fori_loop(0, seq_dev, seq_step, 0)
        if h == heads - 1:
            gain_send(0, jnp.sum(acc[...], axis=1))
        peers(lambda d: fill_back(h, d))
        peers(lambda d: back_copy(h, d, me).start())

    def finish(h):
        peers(lambda d: back_copy(h, d, d).wait_recv())
        for i in range(img_dev):
            cell = home_cell[i]
            cd, cc = lax.div(cell, cap), lax.rem(cell, cap)
            both = jnp.where(home_flag[i] == 1, grads[h][home_slot[i]], homes[h][cd, cc])
            dv_v[i, :, h * hd : (h + 1) * hd] = both[1]
            dy = both[0].astype(F32)
            x = own_k[i, :, h * hd : (h + 1) * hd].astype(F32)
            r = lax.rsqrt(jnp.mean(x * x, axis=-1, keepdims=True) + 1e-05)
            u = kg * dy
            xr = x * r
            dk_v[i, :, h * hd : (h + 1) * hd] = (
                r * (u - xr * jnp.mean(xr * u, axis=-1, keepdims=True))
            ).astype(BF16)

    gain_send(1, gain_recv(0))
    for h in range(heads - 1):
        finish(h)
    gain_send(2, gain_recv(1))
    finish(heads - 1)
    total = gain_recv(2)
    gq_out[...] = total[0:1]
    gk_out[...] = total[1:2]

    peers(lambda d: route_copy(d, me).wait_send())
    for h in range(heads):
        peers(lambda d: kv_copy(h, d, me).wait_send())
        peers(lambda d: back_copy(h, d, me).wait_send())
    for n in range(len(AXES)):
        for o in range(1, sizes[AXES[n]]):
            gain_copy(n, o, lax.axis_index(AXES[n])).wait_send()


def put_out(*refs):
    copies = [pltpu.make_async_copy(refs[n], refs[5 + n], refs[10].at[n]) for n in range(5)]
    for copy in copies:
        copy.start()
    for copy in copies:
        copy.wait()


def on_device(
    queries, cotangent, keys_raw, values, image_counts, image_route, text_lengths, q_gain, k_gain
):
    sizes = {axis: lax.axis_size(axis) for axis in AXES}
    dp = sizes["dp"]
    seq_dev = image_counts.shape[0]
    img_dev, patches, kv_width = keys_raw.shape
    hd = q_gain.shape[0]
    heads = kv_width // hd
    tokens = queries.shape[0]
    seq_len = tokens // seq_dev
    group = queries.shape[1] // hd // heads
    cap = (4 * seq_dev + dp - 1) // dp
    slots = 4 * seq_dev
    rows = group * seq_len
    dims = (seq_dev, seq_len, img_dev, patches, heads, group, hd, cap, sizes)
    cells = (dp, cap, 2, patches, hd)
    vmem, smem, dma = pltpu.VMEM, pltpu.SMEM, pltpu.SemaphoreType.DMA
    unit = (heads, seq_dev, rows, hd)
    scratch = [
        [
            vmem(queries.shape, BF16),
            vmem(queries.shape, BF16),
            vmem(keys_raw.shape, BF16),
            vmem(keys_raw.shape, BF16),
            vmem(unit, F32),
            vmem(unit, F32),
            vmem(unit, BF16),
            vmem(unit, BF16),
            smem((seq_dev,), jnp.int32),
            smem((img_dev,), jnp.int32),
            smem((seq_dev,), jnp.int32),
            vmem((2, 8, hd), F32),
            vmem((1, 128), jnp.int32),
            vmem((dp, 1, 128), jnp.int32),
            smem((dp, 1, 128), jnp.int32),
            smem((slots,), jnp.int32),
            smem((slots,), jnp.int32),
            smem((slots,), jnp.int32),
            smem((dp * cap,), jnp.int32),
            smem((img_dev,), jnp.int32),
            smem((img_dev,), jnp.int32),
            smem((img_dev,), jnp.int32),
            vmem((1, hd), F32),
            vmem((1, hd), F32),
        ],
        [vmem(cells, BF16) for _ in range(heads)],
        [vmem(cells, BF16) for _ in range(heads)],
        [vmem((slots, 2, patches, hd), BF16) for _ in range(heads)],
        [vmem(cells, BF16) for _ in range(heads)],
        [vmem(cells, BF16) for _ in range(heads)],
        vmem((len(AXES), 2, hd), F32),
        [vmem((sizes[a], 2, hd), F32) for a in AXES],
        [
            dma((9,)),
            dma((dp,)),
            dma((dp,)),
            dma((dp,)),
            dma((heads, dp)),
            dma((heads, dp)),
            dma((heads, dp)),
            dma((heads, dp)),
        ],
        [dma((sizes[a],)) for a in AXES for _ in range(2)],
    ]
    hbm = pl.BlockSpec(memory_space=pl.ANY)
    in_vmem = pl.BlockSpec(memory_space=pltpu.VMEM)
    shapes = (
        (queries.shape, BF16),
        (keys_raw.shape, BF16),
        (values.shape, BF16),
        ((1, hd), F32),
        ((1, hd), F32),
    )
    operands = (
        queries,
        cotangent,
        keys_raw,
        values,
        image_counts,
        image_route,
        text_lengths,
        q_gain.reshape(1, hd),
        k_gain.reshape(1, hd),
    )
    results = pl.pallas_call(
        functools.partial(fused, dims),
        out_shape=tuple(pltpu.VMEM(shape, dtype) for shape, dtype in shapes),
        in_specs=[pl.BlockSpec(memory_space=pltpu.HBM)] * 9,
        out_specs=(in_vmem,) * 5,
        scratch_shapes=scratch,
        compiler_params=pltpu.CompilerParams(collective_id=0, has_side_effects=True, vmem_limit_bytes=40 * 2**20),
        name="relay_attention",
    )(*[pltpu.with_memory_space_constraint(x, pltpu.HBM) for x in operands])
    query_grad, key_grad, value_grad, gq, gk = pl.pallas_call(
        put_out,
        out_shape=tuple(jax.ShapeDtypeStruct(shape, dtype) for shape, dtype in shapes),
        in_specs=[hbm] * 5,
        out_specs=(hbm,) * 5,
        scratch_shapes=[dma((5,))],
        compiler_params=pltpu.CompilerParams(vmem_limit_bytes=2**20),
        name="put_out",
    )(*results)
    return (query_grad, key_grad, value_grad, gq.reshape(hd), gk.reshape(hd))


def solution(mesh):
    placed = (
        P(("sec", "dp"), "mp"),
        P(("sec", "dp"), "mp"),
        P(("sec", "dp"), None, "mp"),
        P(("sec", "dp"), None, "mp"),
        P(("sec", "dp")),
        P(("sec", "dp")),
        P(("sec", "dp")),
        P(),
        P(),
    )
    return jax.shard_map(
        on_device,
        mesh=mesh,
        in_specs=placed,
        out_specs=(
            P(("sec", "dp"), "mp"),
            P(("sec", "dp"), None, "mp"),
            P(("sec", "dp"), None, "mp"),
            P(),
            P(),
        ),
        check_vma=False,
    )
```

```python
import functools

import jax
import jax.numpy as jnp
from jax import lax
from jax.experimental import pallas as pl
from jax.experimental.pallas import tpu as pltpu
from jax.sharding import PartitionSpec as P

MESH = pl.DeviceIdType.MESH
AXES = ("dp", "mp", "sec")
PLANE, LINE = 0, 1
F32 = jnp.float32
BF16 = jnp.bfloat16


def dot(a, b, ca, cb):
    return lax.dot_general(a, b, (((ca,), (cb,)), ((), ())), preferred_element_type=F32)


def fold_rows(x):
    return jnp.sum(x.reshape(x.shape[0] // 8, 8, x.shape[1]), axis=0)


def fused(
    dims,
    q_hbm,
    c_hbm,
    k_hbm,
    v_hbm,
    counts_hbm,
    route_hbm,
    lens_hbm,
    q_gain_hbm,
    k_gain_hbm,
    dq_v,
    dk_v,
    dv_v,
    gq_out,
    gk_out,
    bufs,
    sends,
    recvs,
    grads,
    backs,
    homes,
    parts,
    gathers,
    sems,
    gain_sems,
    from_left,
    from_right,
):
    seq_dev, seq_len, img_dev, patches, heads, group, hd, cap, sizes = dims
    (q_v, c_v, own_k, own_v, xhat_v, rinv_v, qn_v, gr_v, counts, route, lens) = bufs[:11]
    q_gain, k_gain = bufs[22:]
    (acc, route_out, route_in, route_s, slot_own, slot_cell, slot_flag, cell_slot,
     home_slot, home_cell, home_flag) = bufs[11:22]
    (in_sem, rt_send, rt_recv, rt_local, kv_send, kv_recv, bk_send, bk_recv) = sems
    dp = sizes["dp"]
    me = lax.axis_index("dp")
    scaling = hd ** (-0.5)
    slots = 4 * seq_dev
    first_code = (lax.axis_index("sec") * dp + me) * slots

    def peer(axis, offset):
        return lax.rem(lax.axis_index(axis) + offset, sizes[axis])

    barrier = pltpu.get_barrier_semaphore()
    line_me, line_n = lax.axis_index("mp"), sizes["mp"]
    plane_n = dp * sizes["sec"]
    has_left, has_right = line_me > 0, line_me < line_n - 1

    def plane_id(o):
        return {"dp": peer("dp", lax.rem(o, dp)), "sec": peer("sec", lax.div(o, dp))}

    def plane_slot(where):
        return where["sec"] * dp + where["dp"]

    def plane_peers(body):
        if plane_n <= 8:
            for o in range(1, plane_n):
                body(plane_id(jnp.int32(o)))
        else:

            def step(o, carry):
                body(plane_id(o))
                return carry

            lax.fori_loop(1, plane_n, step, 0)

    def tell(sem, where):
        pl.semaphore_signal(sem, inc=1, device_id=where, device_id_type=MESH)

    plane_peers(lambda where: tell(barrier, where))
    pl.when(has_left)(lambda: tell(barrier, {"mp": line_me - 1}))
    pl.when(has_right)(lambda: tell(barrier, {"mp": line_me + 1}))

    in_copies = [
        pltpu.make_async_copy(src, dst, in_sem.at[n])
        for n, (src, dst) in enumerate(
            (
                (route_hbm, route),
                (k_hbm, own_k),
                (v_hbm, own_v),
                (q_hbm, q_v),
                (c_hbm, c_v),
                (counts_hbm, counts),
                (lens_hbm, lens),
                (q_gain_hbm, q_gain),
                (k_gain_hbm, k_gain),
            )
        )
    ]
    for copy in in_copies:
        copy.start()

    lane = lax.broadcasted_iota(jnp.int32, (1, 128), 1)
    in_copies[0].wait()
    codes = [route[i] for i in range(img_dev)]
    packed = jnp.zeros((1, 128), jnp.int32)
    for i in range(img_dev):
        packed = jnp.where(lane == i, codes[i], packed)
    route_out[...] = packed
    target = [lax.rem(lax.div(codes[i], slots), dp) for i in range(img_dev)]

    for i in range(img_dev):
        order = jnp.int32(0)
        for j in range(i):
            order = order + jnp.where(target[j] == target[i], 1, 0)
        mine = target[i] == me
        home_flag[i] = jnp.where(mine, 1, 0)
        home_slot[i] = jnp.where(mine, jnp.clip(codes[i] - first_code, 0, slots - 1), 0)
        home_cell[i] = jnp.where(mine, peer("dp", 1) * cap, target[i] * cap + jnp.minimum(order, cap - 1))

    def send_cells(h, d):
        for c in range(cap):
            image = jnp.int32(0)
            for i in range(img_dev):
                image = jnp.where(home_cell[i] == d * cap + c, jnp.where(target[i] == d, i, image), image)
            sends[h][d, c, 0] = own_k[image, :, h * hd : (h + 1) * hd]
            sends[h][d, c, 1] = own_v[image, :, h * hd : (h + 1) * hd]

    def kv_copy(h, d, slot):
        return pltpu.make_async_remote_copy(
            src_ref=sends[h].at[d],
            dst_ref=recvs[h].at[slot],
            send_sem=kv_send.at[h, d],
            recv_sem=kv_recv.at[h, slot],
            device_id={"dp": d},
            device_id_type=MESH,
        )

    def back_copy(h, d, slot):
        return pltpu.make_async_remote_copy(
            src_ref=backs[h].at[d],
            dst_ref=homes[h].at[slot],
            send_sem=bk_send.at[h, d],
            recv_sem=bk_recv.at[h, slot],
            device_id={"dp": d},
            device_id_type=MESH,
        )

    def route_copy(d, slot):
        return pltpu.make_async_remote_copy(
            src_ref=route_out,
            dst_ref=route_in.at[slot],
            send_sem=rt_send.at[d],
            recv_sem=rt_recv.at[slot],
            device_id={"dp": d},
            device_id_type=MESH,
        )

    def peers(body):
        if dp == 2:
            body(peer("dp", 1))
        else:

            def step(o, carry):
                body(peer("dp", o))
                return carry

            lax.fori_loop(1, dp, step, 0)

    in_copies[1].wait()
    in_copies[2].wait()
    peers(lambda d: send_cells(0, d))
    pl.semaphore_wait(
        barrier, plane_n - 1 + jnp.where(has_left, 1, 0) + jnp.where(has_right, 1, 0)
    )
    peers(lambda d: route_copy(d, me).start())
    peers(lambda d: kv_copy(0, d, me).start())
    for h in range(1, heads):
        peers(lambda d: send_cells(h, d))
        peers(lambda d: kv_copy(h, d, me).start())

    for copy in in_copies[3:]:
        copy.wait()
    qg = q_gain[...]
    kg = k_gain[...]
    rows = group * seq_len
    row_token = lax.rem(lax.broadcasted_iota(jnp.int32, (rows, 1), 0), seq_len)

    def stack(ref, s, h):
        return jnp.concatenate(
            [
                ref[pl.ds(pl.multiple_of(s * seq_len, seq_len), seq_len), (h * group + g) * hd : (h * group + g + 1) * hd]
                for g in range(group)
            ],
            axis=0,
        )

    def prepare(s, carry):
        for h in range(heads):
            x = stack(q_v, s, h).astype(F32)
            r = lax.rsqrt(jnp.mean(x * x, axis=-1, keepdims=True) + 1e-05)
            xr = x * r
            xhat_v[h, s] = xr
            rinv_v[h, s] = jnp.broadcast_to(r, xr.shape)
            qn_v[h, s] = (xr * qg).astype(BF16)
            grad = stack(c_v, s, h)
            gr_v[h, s] = jnp.where(row_token < lens[s], grad, jnp.zeros_like(grad))
        return carry

    lax.fori_loop(0, seq_dev, prepare, 0)
    acc[...] = jnp.zeros_like(acc)
    pl.when(has_left)(lambda: pl.semaphore_wait(from_left, 1))
    pl.when(has_right)(lambda: tell(from_left, {"mp": line_me + 1}))
    pl.when(has_right)(lambda: pl.semaphore_wait(from_right, 1))
    pl.when(has_left)(lambda: tell(from_right, {"mp": line_me - 1}))

    for q in range(slots):
        own = jnp.int32(0)
        flag = jnp.int32(0)
        for i in range(img_dev):
            match = codes[i] - first_code == q
            own = jnp.where(match, i, own)
            flag = jnp.where(match, 1, flag)
        slot_own[q] = own
        slot_flag[q] = flag
        slot_cell[q] = peer("dp", 1) * cap

    peers(lambda d: route_copy(d, d).wait_recv())
    peers(lambda d: pltpu.make_async_copy(route_in.at[d], route_s.at[d], rt_local.at[d]).start())
    peers(lambda d: pltpu.make_async_copy(route_in.at[d], route_s.at[d], rt_local.at[d]).wait())

    def scan_source(d):
        run = jnp.int32(0)
        local, place = [], []
        for i in range(img_dev):
            code = route_s[d, 0, i] - first_code
            mine = (code >= 0) & (code < slots)
            local.append(jnp.where(mine, code, -1))
            place.append(jnp.where(mine, jnp.minimum(run, cap - 1), -1))
            run = run + jnp.where(mine, 1, 0)
        for q in range(slots):
            cell = slot_cell[q]
            for i in range(img_dev):
                cell = jnp.where(local[i] == q, d * cap + place[i], cell)
            slot_cell[q] = cell
        for c in range(cap):
            slot = jnp.int32(0)
            for i in range(img_dev):
                slot = jnp.where(place[i] == c, local[i], slot)
            cell_slot[d * cap + c] = slot

    peers(scan_source)

    keys = 4 * patches
    col_image = lax.div(lax.broadcasted_iota(jnp.int32, (1, keys), 1), patches)

    def attend(h, s):
        raw, val = [], []
        for p in range(4):
            n = 4 * s + p
            own, cell = slot_own[n], slot_cell[n]
            mine = slot_flag[n] == 1
            live = p < counts[s]
            cd, cc = lax.div(cell, cap), lax.rem(cell, cap)
            k_one = jnp.where(mine, own_k[own, :, h * hd : (h + 1) * hd], recvs[h][cd, cc, 0])
            v_one = jnp.where(mine, own_v[own, :, h * hd : (h + 1) * hd], recvs[h][cd, cc, 1])
            raw.append(jnp.where(live, k_one, jnp.zeros_like(k_one)))
            val.append(jnp.where(live, v_one, jnp.zeros_like(v_one)))
        kx = jnp.concatenate(raw, axis=0).astype(F32)
        v = jnp.concatenate(val, axis=0)
        kx = kx * lax.rsqrt(jnp.mean(kx * kx, axis=-1, keepdims=True) + 1e-05)
        kn = (kx * kg).astype(BF16)
        qn = qn_v[h, s]
        grad = gr_v[h, s]
        scores = jnp.where(col_image < counts[s], dot(qn, kn, 1, 1) * scaling, -1e30)
        dprob = dot(grad, v, 1, 1)
        expo = jnp.exp(scores - jnp.max(scores, axis=-1, keepdims=True))
        probs = expo * (1.0 / jnp.sum(expo, axis=-1, keepdims=True))
        low = probs.astype(BF16)
        row_dots = jnp.sum(low.astype(F32) * dprob, axis=-1, keepdims=True)
        dscore = (probs * (dprob - row_dots)).astype(BF16)
        dv = dot(low, grad, 0, 0).astype(BF16)
        dk = (dot(dscore, qn, 0, 0) * scaling).astype(BF16)
        dq = dot(dscore, kn, 1, 0) * scaling
        for p in range(4):
            grads[h][4 * s + p, 0] = dk[p * patches : (p + 1) * patches]
            grads[h][4 * s + p, 1] = dv[p * patches : (p + 1) * patches]
        acc[1] += fold_rows(dk.astype(F32) * kx)
        xr = xhat_v[h, s]
        prod = xr * dq
        acc[0] += fold_rows(prod)
        mean = jnp.mean(prod * qg, axis=-1, keepdims=True)
        dx = (rinv_v[h, s] * (dq * qg - xr * mean)).astype(BF16)
        for g in range(group):
            dq_v[
                pl.ds(pl.multiple_of(s * seq_len, seq_len), seq_len),
                (h * group + g) * hd : (h * group + g + 1) * hd,
            ] = dx[g * seq_len : (g + 1) * seq_len]

    def fill_back(h, d):
        for c in range(cap):
            slot = cell_slot[d * cap + c]
            backs[h][d, c] = grads[h][slot]

    def plane_copy(where, slot):
        return pltpu.make_async_remote_copy(
            src_ref=parts.at[PLANE],
            dst_ref=gathers[PLANE].at[slot],
            send_sem=gain_sems[0].at[plane_slot(where)],
            recv_sem=gain_sems[1].at[slot],
            device_id=where,
            device_id_type=MESH,
        )

    def line_copy(o, slot):
        return pltpu.make_async_remote_copy(
            src_ref=parts.at[LINE],
            dst_ref=gathers[LINE].at[slot],
            send_sem=gain_sems[2].at[o],
            recv_sem=gain_sems[3].at[slot],
            device_id={"mp": peer("mp", o)},
            device_id_type=MESH,
        )

    plane_me = plane_slot({"dp": me, "sec": lax.axis_index("sec")})

    def plane_send(value):
        parts[PLANE] = value
        gathers[PLANE][plane_me] = value
        plane_peers(lambda where: plane_copy(where, plane_me).start())

    def plane_recv():
        plane_peers(lambda where: plane_copy(where, plane_slot(where)).wait_recv())
        return jnp.sum(gathers[PLANE][...], axis=0)

    def line_send(value):
        parts[LINE] = value
        gathers[LINE][line_me] = value
        for o in range(1, line_n):
            line_copy(o, line_me).start()

    def line_recv():
        for o in range(1, line_n):
            line_copy(o, peer("mp", o)).wait_recv()
        return jnp.sum(gathers[LINE][...], axis=0)

    for h in range(heads):
        peers(lambda d: kv_copy(h, d, d).wait_recv())

        def seq_step(s, carry):
            attend(h, s)
            return carry

        lax.fori_loop(0, seq_dev, seq_step, 0)
        if h == heads - 1:
            plane_send(jnp.sum(acc[...], axis=1))
        peers(lambda d: fill_back(h, d))
        peers(lambda d: back_copy(h, d, me).start())

    def finish(h):
        peers(lambda d: back_copy(h, d, d).wait_recv())
        for i in range(img_dev):
            cell = home_cell[i]
            cd, cc = lax.div(cell, cap), lax.rem(cell, cap)
            both = jnp.where(home_flag[i] == 1, grads[h][home_slot[i]], homes[h][cd, cc])
            dv_v[i, :, h * hd : (h + 1) * hd] = both[1]
            dy = both[0].astype(F32)
            x = own_k[i, :, h * hd : (h + 1) * hd].astype(F32)
            r = lax.rsqrt(jnp.mean(x * x, axis=-1, keepdims=True) + 1e-05)
            u = kg * dy
            xr = x * r
            dk_v[i, :, h * hd : (h + 1) * hd] = (
                r * (u - xr * jnp.mean(xr * u, axis=-1, keepdims=True))
            ).astype(BF16)

    for h in range(heads - 1):
        finish(h)
    line_send(plane_recv())
    finish(heads - 1)
    total = line_recv()
    gq_out[...] = total[0:1]
    gk_out[...] = total[1:2]

    peers(lambda d: route_copy(d, me).wait_send())
    for h in range(heads):
        peers(lambda d: kv_copy(h, d, me).wait_send())
        peers(lambda d: back_copy(h, d, me).wait_send())
    plane_peers(lambda where: plane_copy(where, plane_me).wait_send())
    for o in range(1, line_n):
        line_copy(o, line_me).wait_send()


def put_out(*refs):
    copies = [pltpu.make_async_copy(refs[n], refs[5 + n], refs[10].at[n]) for n in range(5)]
    for copy in copies:
        copy.start()
    for copy in copies:
        copy.wait()


def on_device(
    queries, cotangent, keys_raw, values, image_counts, image_route, text_lengths, q_gain, k_gain
):
    sizes = {axis: lax.axis_size(axis) for axis in AXES}
    dp = sizes["dp"]
    seq_dev = image_counts.shape[0]
    img_dev, patches, kv_width = keys_raw.shape
    hd = q_gain.shape[0]
    heads = kv_width // hd
    tokens = queries.shape[0]
    seq_len = tokens // seq_dev
    group = queries.shape[1] // hd // heads
    cap = (4 * seq_dev + dp - 1) // dp
    slots = 4 * seq_dev
    rows = group * seq_len
    dims = (seq_dev, seq_len, img_dev, patches, heads, group, hd, cap, sizes)
    cells = (dp, cap, 2, patches, hd)
    vmem, smem, dma = pltpu.VMEM, pltpu.SMEM, pltpu.SemaphoreType.DMA
    unit = (heads, seq_dev, rows, hd)
    scratch = [
        [
            vmem(queries.shape, BF16),
            vmem(queries.shape, BF16),
            vmem(keys_raw.shape, BF16),
            vmem(keys_raw.shape, BF16),
            vmem(unit, F32),
            vmem(unit, F32),
            vmem(unit, BF16),
            vmem(unit, BF16),
            smem((seq_dev,), jnp.int32),
            smem((img_dev,), jnp.int32),
            smem((seq_dev,), jnp.int32),
            vmem((2, 8, hd), F32),
            vmem((1, 128), jnp.int32),
            vmem((dp, 1, 128), jnp.int32),
            smem((dp, 1, 128), jnp.int32),
            smem((slots,), jnp.int32),
            smem((slots,), jnp.int32),
            smem((slots,), jnp.int32),
            smem((dp * cap,), jnp.int32),
            smem((img_dev,), jnp.int32),
            smem((img_dev,), jnp.int32),
            smem((img_dev,), jnp.int32),
            vmem((1, hd), F32),
            vmem((1, hd), F32),
        ],
        [vmem(cells, BF16) for _ in range(heads)],
        [vmem(cells, BF16) for _ in range(heads)],
        [vmem((slots, 2, patches, hd), BF16) for _ in range(heads)],
        [vmem(cells, BF16) for _ in range(heads)],
        [vmem(cells, BF16) for _ in range(heads)],
        vmem((2, 2, hd), F32),
        [vmem((dp * sizes["sec"], 2, hd), F32), vmem((sizes["mp"], 2, hd), F32)],
        [
            dma((9,)),
            dma((dp,)),
            dma((dp,)),
            dma((dp,)),
            dma((heads, dp)),
            dma((heads, dp)),
            dma((heads, dp)),
            dma((heads, dp)),
        ],
        [dma((n,)) for n in (dp * sizes["sec"], sizes["mp"]) for _ in range(2)],
        pltpu.SemaphoreType.REGULAR,
        pltpu.SemaphoreType.REGULAR,
    ]
    hbm = pl.BlockSpec(memory_space=pl.ANY)
    in_vmem = pl.BlockSpec(memory_space=pltpu.VMEM)
    shapes = (
        (queries.shape, BF16),
        (keys_raw.shape, BF16),
        (values.shape, BF16),
        ((1, hd), F32),
        ((1, hd), F32),
    )
    operands = (
        queries,
        cotangent,
        keys_raw,
        values,
        image_counts,
        image_route,
        text_lengths,
        q_gain.reshape(1, hd),
        k_gain.reshape(1, hd),
    )
    results = pl.pallas_call(
        functools.partial(fused, dims),
        out_shape=tuple(pltpu.VMEM(shape, dtype) for shape, dtype in shapes),
        in_specs=[pl.BlockSpec(memory_space=pltpu.HBM)] * 9,
        out_specs=(in_vmem,) * 5,
        scratch_shapes=scratch,
        compiler_params=pltpu.CompilerParams(collective_id=0, has_side_effects=True, vmem_limit_bytes=40 * 2**20),
        name="relay_attention",
    )(*[pltpu.with_memory_space_constraint(x, pltpu.HBM) for x in operands])
    query_grad, key_grad, value_grad, gq, gk = pl.pallas_call(
        put_out,
        out_shape=tuple(jax.ShapeDtypeStruct(shape, dtype) for shape, dtype in shapes),
        in_specs=[hbm] * 5,
        out_specs=(hbm,) * 5,
        scratch_shapes=[dma((5,))],
        compiler_params=pltpu.CompilerParams(vmem_limit_bytes=2**20),
        name="put_out",
    )(*results)
    return (query_grad, key_grad, value_grad, gq.reshape(hd), gk.reshape(hd))


def solution(mesh):
    placed = (
        P(("sec", "dp"), "mp"),
        P(("sec", "dp"), "mp"),
        P(("sec", "dp"), None, "mp"),
        P(("sec", "dp"), None, "mp"),
        P(("sec", "dp")),
        P(("sec", "dp")),
        P(("sec", "dp")),
        P(),
        P(),
    )
    return jax.shard_map(
        on_device,
        mesh=mesh,
        in_specs=placed,
        out_specs=(
            P(("sec", "dp"), "mp"),
            P(("sec", "dp"), None, "mp"),
            P(("sec", "dp"), None, "mp"),
            P(),
            P(),
        ),
        check_vma=False,
    )
```
